32 devices in a mesh: grid: 8 (over z, y), vis: 4 (over x, core).
Axes of the slice: x: 2, y: 2, z: 4, core: 2. Of those that a mesh axis runs over, the one named last changes fastest.
Arguments:
- vis_coords: float32 [8, 256, 2, 512], P('grid', 'vis'), may hold values from 0 to 64
- vis_values: float32 [8, 256, 2, 512], P('grid', 'vis'), may hold values from -6 to 6
- tile_index: int32 [8, 256], P('grid', 'vis'), may hold values from 0 to 63
Outputs:
- facets: float32 [8, 2, 1024, 1024], P('grid', None, 'vis')
The draws below stay inside these ranges and needn't reach their ends.
Inputs may be any that keep to these rules, and one draw needn't show every extreme that they name: `tile_index`: tile a * 8 + e covers subgrid rows from a * 64 and columns from e * 64.
All inputs are finite; a program needn't handle non-finite values.
Results may differ from the reference program's by a relative error of at most 0.014.
Values may be sent and summed in bfloat16 or wider, within the bound.
A program may use at most 64 MiB of HBM per device.

```python
import math
import jax
import jax.numpy as jnp
from jax import lax

SUB = 512
FAC = 1024
CONTRIB = 64
TILE = 64
BLK = 512
BLK_DEV = 64
NBLK = 8
VBLOCKS = 256
SUBGRIDS = 8
N_GRID = 8
N_VIS = 4


def touch_ends(entries, stream_key, least, high):
    shape = entries.shape
    index_at = [jax.random.randint(jax.random.fold_in(stream_key, axis), (), 0, shape[axis]) for axis in range(len(shape))]
    entries = entries.at[tuple(index_at)].set(least)
    longest = shape.index(max(shape))
    index_at[longest] = (index_at[longest] + 1) % shape[longest]
    return entries.at[tuple(index_at)].set(high)


def block_scale(stream_key, shape, split, smallest, largest):
    loudness, own = 1.0, jax.random.fold_in(stream_key, 6)
    for position, shards_of in split:
        heights = jnp.exp(jax.random.uniform(jax.random.fold_in(own, position), (shards_of,), jnp.float32, smallest / len(split), largest / len(split)))
        loudness = loudness * jnp.repeat(heights, shape[position] // shards_of).reshape([-1 if axis == position else 1 for axis in range(len(shape))])
    return loudness


def noise(key, dims, width, reach, pieces=(), kind=jnp.bfloat16):
    result = jax.random.normal(key, dims, jnp.float32) * width
    if len(pieces) > 0:
        result = block_scale(key, dims, pieces, -0.22, 0.18) * result
    return jnp.clip(result, min=-reach, max=reach).astype(kind)


def setup_inputs(seed: int = 0) -> dict:
    seeds = jax.random.split(jax.random.key(seed), 4)
    vis_coords = jnp.clip(64.0 * jax.random.uniform(seeds[0], (SUBGRIDS, VBLOCKS, 2, BLK), jnp.float32) ** block_scale(seeds[0], (SUBGRIDS, VBLOCKS, 2, BLK), ((0, 8), (1, 4)), -0.2, 0.2), 0.0, 64.0)
    vis_values = noise(seeds[1], (SUBGRIDS, VBLOCKS, 2, BLK), 1.0, 6.0, ((0, 8), (1, 4)), jnp.float32)
    tile_index = touch_ends(jax.random.randint(seeds[2], (SUBGRIDS, VBLOCKS), 0, (SUB // TILE) * (SUB // TILE)), jax.random.fold_in(seeds[2], 1), 0, ((SUB // TILE) * (SUB // TILE)) - 1).astype(jnp.int32)
    return dict(vis_coords=vis_coords, vis_values=vis_values, tile_index=tile_index)


taper_scale = 16.0

def phase_pair(frequencies, points, length):
    phases = frequencies[:, None] * points[None, :] % length
    angles = phases.astype(jnp.float32) * (2.0 * math.pi / length)
    return (jnp.cos(angles), jnp.sin(angles))

def kernel_rows(places):
    pixels = jnp.arange(TILE, dtype=jnp.float32)
    distance = pixels - places[..., None]
    scaled = distance / taper_scale
    return jnp.sinc(distance) * jnp.exp(-scaled * scaled)

def exact_dot(first, second):
    return jnp.dot(first.astype(jnp.float32), second.astype(jnp.float32), precision=lax.Precision.HIGHEST, preferred_element_type=jnp.float32)

def grid_blocks(coords, values, tile_ids):
    across = SUB // TILE
    weights_u = kernel_rows(coords[:, 0])
    weights_v = kernel_rows(coords[:, 1])
    weighted = weights_u[:, None] * values[:, :, :, None]
    patches = jnp.einsum('bcnx,bny->bcxy', weighted, weights_v, precision=lax.Precision.HIGHEST, preferred_element_type=jnp.float32)
    onehot = (tile_ids[None, :] == jnp.arange(across * across, dtype=jnp.int32)[:, None]).astype(jnp.float32)
    placed = jnp.dot(onehot, patches.reshape(coords.shape[0], 2 * TILE * TILE), precision=lax.Precision.HIGHEST, preferred_element_type=jnp.float32)
    return placed.reshape(across, across, 2, TILE, TILE).transpose(0, 3, 2, 1, 4).reshape(SUB, 2, SUB)

def complex_block(part_real, part_imag):
    return jnp.concatenate([jnp.concatenate([part_real, part_imag], 1), jnp.concatenate([-part_imag, part_real], 1)], 0)

def reference(vis_coords, vis_values, tile_index):
    groups = N_GRID // NBLK
    column_count = groups * CONTRIB
    unitary = 1.0 / math.sqrt(SUB)
    spectrum = jnp.arange(SUB, dtype=jnp.int32)
    tab_real, tab_imag = phase_pair(spectrum, jnp.arange(column_count, dtype=jnp.int32), SUB)
    col_table = jnp.concatenate([jnp.concatenate([tab_real, -tab_imag], 1), jnp.concatenate([tab_imag, tab_real], 1)], 0).astype(jnp.bfloat16)
    rows_real, rows_imag = phase_pair(spectrum, spectrum, SUB)
    left_side = jnp.concatenate([rows_real, -rows_imag], 1).astype(jnp.bfloat16)

    def one_subgrid(inputs):
        coords, values, tile_ids = inputs
        running = jnp.zeros((SUB, 2, SUB), jnp.float32)
        for member in range(N_VIS):
            first = member * BLK_DEV
            placed = grid_blocks(coords[first:first + BLK_DEV], values[first:first + BLK_DEV], tile_ids[first:first + BLK_DEV])
            running = running + lax.optimization_barrier(placed.astype(jnp.bfloat16)).astype(jnp.float32)
        summed = running.astype(jnp.bfloat16)
        images = (exact_dot(summed.reshape(SUB, 2 * SUB), col_table) * unitary).astype(jnp.bfloat16).reshape(SUB, 2, column_count)
        stacked = complex_block(images[:, 0], images[:, 1])
        spectra = (exact_dot(left_side, stacked) * unitary).astype(jnp.bfloat16)
        return spectra.reshape(NBLK, CONTRIB, 2, groups, CONTRIB).transpose(3, 0, 2, 1, 4).reshape(N_GRID, 2, CONTRIB, CONTRIB)
    contribs = lax.map(one_subgrid, (vis_coords, vis_values, tile_index))
    embed_real, embed_imag = phase_pair(jnp.arange(FAC, dtype=jnp.int32), spectrum, FAC)
    embed_left = jnp.concatenate([embed_real, embed_imag], 1).astype(jnp.bfloat16)
    out_real, out_imag = phase_pair(jnp.arange(column_count, dtype=jnp.int32), jnp.arange(FAC, dtype=jnp.int32), FAC)
    real_right = jnp.concatenate([out_real, -out_imag], 0).astype(jnp.bfloat16)
    imag_right = jnp.concatenate([out_imag, out_real], 0).astype(jnp.bfloat16)
    sines = jnp.sin(math.pi * (jnp.arange(FAC, dtype=jnp.float32) + 0.5) / FAC)
    taper_rows = 0.25 + 0.75 * sines * sines
    weight = taper_rows[:, None] * taper_rows[None, :] * (1.0 / math.sqrt(CONTRIB * groups))

    def one_facet(facet_id):
        received = lax.dynamic_index_in_dim(contribs, facet_id, 1, keepdims=False)
        blocks = received.reshape(groups, NBLK, 2, CONTRIB, CONTRIB).transpose(1, 3, 2, 0, 4)
        part_real = blocks[:, :, 0].reshape(SUB, column_count)
        part_imag = blocks[:, :, 1].reshape(SUB, column_count)
        mixture = (exact_dot(embed_left, complex_block(part_real, part_imag)) * unitary).astype(jnp.bfloat16)
        return jnp.stack([exact_dot(mixture, real_right) * weight, exact_dot(mixture, imag_right) * weight])
    return lax.map(one_facet, jnp.arange(N_GRID, dtype=jnp.int32))
```

```python
import functools
import math

import jax
import jax.numpy as jnp
import ml_dtypes
import numpy as np
from jax import lax
from jax.experimental import pallas as pl
from jax.experimental.pallas import tpu as pltpu
from jax.sharding import PartitionSpec as P

SUB = 512
FAC = 1024
CONTRIB = 64
TILE = 64
NBLK = 8
LANES = 2 * CONTRIB
TAPER_SCALE = 16.0
MESH = pl.DeviceIdType.MESH


def phase_pair(frequencies, points, length):
    phases = (frequencies[:, None] * points[None, :]) % length
    angles = phases * (2.0 * math.pi / length)
    return np.cos(angles).astype(np.float32), np.sin(angles).astype(np.float32)


def as_bf16(array):
    return array.astype(ml_dtypes.bfloat16)


def column_table(groups):
    cos, sin = phase_pair(np.arange(SUB), np.arange(groups * CONTRIB), SUB)
    across = SUB // TILE
    table = np.zeros((across, 2, TILE, groups, 4, CONTRIB), np.float32)
    cos = cos.reshape(across, TILE, groups, CONTRIB)
    sin = sin.reshape(across, TILE, groups, CONTRIB)
    table[:, 0, :, :, 0], table[:, 1, :, :, 0] = cos, sin
    table[:, 0, :, :, 1], table[:, 1, :, :, 1] = -sin, cos
    table[:, :, :, :, 2] = -table[:, :, :, :, 1]
    table[:, :, :, :, 3] = table[:, :, :, :, 0]
    return as_bf16(table.reshape(2 * SUB, groups * 4 * CONTRIB))


def row_table(vis_count):
    quarter = CONTRIB // vis_count
    order = np.arange(SUB).reshape(NBLK, vis_count, quarter).transpose(1, 0, 2).reshape(SUB)
    cos, sin = phase_pair(order, np.arange(SUB), SUB)
    return as_bf16(np.concatenate([cos, -sin], 1))


def embed_table():
    cos, sin = phase_pair(np.arange(FAC), np.arange(SUB), FAC)
    return as_bf16(np.concatenate([cos, sin], 1))


def output_table(groups):
    cos, sin = phase_pair(np.arange(groups * CONTRIB), np.arange(FAC), FAC)
    cos = cos.reshape(groups, CONTRIB, FAC)
    sin = sin.reshape(groups, CONTRIB, FAC)
    real = np.stack([cos, -sin], 1).reshape(groups * LANES, FAC)
    imag = np.stack([sin, cos], 1).reshape(groups * LANES, FAC)
    return as_bf16(np.concatenate([real, imag], 1))


def taper():
    sines = np.sin(np.pi * (np.arange(FAC) + 0.5) / FAC)
    return 0.25 + 0.75 * sines * sines


SINE = [(-1.0) ** k * math.pi ** (2 * k) / math.factorial(2 * k + 1) for k in range(7)]


def grid_kernel(tiles, coords, values, out, total):
    blocks = coords.shape[0]
    total[...] = jnp.zeros_like(total)
    pixel = lax.broadcasted_iota(jnp.int32, (TILE, 1), 0)
    place = pixel.astype(jnp.float32)
    flip = 1.0 - 2.0 * (pixel % 2).astype(jnp.float32)

    def block(b, carry):
        where = coords[b]
        nearest = jnp.floor(where + 0.5)
        offset = where - nearest
        offset = jnp.where(offset == 0.0, 1e-30, offset)
        square = offset * offset
        wave = jnp.full_like(square, SINE[6])
        for k in range(5, -1, -1):
            wave = wave * square + SINE[k]
        half = nearest * 0.5
        odd = (half - jnp.floor(half)) * 4.0 - 1.0
        wave = wave * offset * odd

        def rows(axis):
            distance = (place - nearest[axis : axis + 1]) - offset[axis : axis + 1]
            near = pl.reciprocal(distance, approx=True)
            near = near * (2.0 - distance * near)
            fall = jnp.exp(distance * distance * (-1.0 / (TAPER_SCALE * TAPER_SCALE)))
            return (flip * wave[axis : axis + 1]) * fall * near

        along = rows(0).astype(jnp.bfloat16)
        down = rows(1)
        data = values[b]
        right = jnp.concatenate([down * data[0:1], down * data[1:2]], 0).astype(jnp.bfloat16)
        patch = lax.dot_general(
            along, right, (((1,), (1,)), ((), ())), preferred_element_type=jnp.float32
        )
        tile = tiles[0, b]
        r = pl.ds(pl.multiple_of(tile // (SUB // TILE) * TILE, TILE), TILE)
        c = pl.ds(pl.multiple_of(tile % (SUB // TILE) * (2 * TILE), 2 * TILE), 2 * TILE)
        total[r, c] += patch
        return carry

    lax.fori_loop(0, blocks, block, 0, unroll=4)
    out[...] = total[...].astype(jnp.bfloat16)


def swapped(index, bits):
    result = index
    bit = 1
    while bit <= bits:
        if bits & bit:
            result = result + bit * (1 - 2 * ((index // bit) % 2))
        bit *= 2
    return result


def exchange_kernel(
    grid_count, vis_count, unitary, part_hbm, col_hbm, row_hbm, embed_hbm, scale_hbm, out,
    part, col, row, embed, scale, spectra, pieces, summed, gathered,
    load_sem, send1, recv1, send2, recv2, send3, recv3,
):
    me_g, me_v = lax.axis_index("grid"), lax.axis_index("vis")
    groups = grid_count // NBLK
    rows_here = out.shape[0]
    quarter = CONTRIB // vis_count
    peers_v = [lax.rem(me_v + k, vis_count) for k in range(vis_count)]
    peers_g = [swapped(me_g, k) for k in range(grid_count)]
    mine = pl.ds(pl.multiple_of(me_v * rows_here, rows_here), rows_here)
    loads = [
        pltpu.make_async_copy(src, dst, load_sem.at[i])
        for i, (src, dst) in enumerate(
            [(part_hbm, part), (col_hbm, col), (row_hbm, row),
             (embed_hbm.at[mine], embed), (scale_hbm.at[mine], scale)]
        )
    ]
    for load in loads:
        load.start()
    barrier = pltpu.get_barrier_semaphore()
    for k in range(grid_count - 1, 0, -1):
        pl.semaphore_signal(barrier, inc=1, device_id=(peers_g[k], me_v), device_id_type=MESH)
    for k in range(1, vis_count):
        pl.semaphore_signal(barrier, inc=1, device_id=(me_g, peers_v[k]), device_id_type=MESH)

    loads[0].wait()
    loads[1].wait()
    loads[2].wait()
    for g in range(groups):
        image = jnp.dot(
            part[...], col[:, 2 * LANES * g : 2 * LANES * (g + 1)], preferred_element_type=jnp.float32
        )
        image = (image * unitary).astype(jnp.bfloat16)
        both = jnp.concatenate([image[:, :LANES], image[:, LANES:]], 0)
        result = jnp.dot(row[...], both, preferred_element_type=jnp.float32)
        result = (result * unitary).astype(jnp.bfloat16)
        spectra[:, NBLK * g : NBLK * (g + 1)] = result.reshape(vis_count, NBLK, quarter, LANES)

    pl.semaphore_wait(barrier, grid_count + vis_count - 2)

    def copy1(k):
        return pltpu.make_async_remote_copy(
            src_ref=spectra.at[peers_v[k]], dst_ref=pieces.at[k], send_sem=send1.at[k],
            recv_sem=recv1.at[k], device_id=(me_g, peers_v[k]), device_id_type=MESH,
        )

    def copy2(k):
        return pltpu.make_async_remote_copy(
            src_ref=summed.at[peers_g[k]], dst_ref=gathered.at[me_g, me_v], send_sem=send2.at[k],
            recv_sem=recv2.at[k], device_id=(peers_g[k], me_v), device_id_type=MESH,
        )

    def copy3(k, j):
        spot = gathered.at[peers_g[k], me_v]
        return pltpu.make_async_remote_copy(
            src_ref=spot, dst_ref=spot, send_sem=send3.at[k, j],
            recv_sem=recv3.at[k, j], device_id=(me_g, peers_v[j]), device_id_type=MESH,
        )

    for k in range(1, vis_count):
        copy1(k).start()
    whole = spectra[me_v].astype(jnp.float32)
    for k in range(1, vis_count):
        copy1(k).wait_recv()
        whole = whole + pieces[k].astype(jnp.float32)
    summed[...] = whole.astype(jnp.bfloat16)
    for k in range(grid_count - 1, 0, -1):
        copy2(k).start()
    gathered[me_g, me_v] = summed[me_g]
    for k in range(grid_count):
        if k > 0:
            copy2(k).wait_recv()
        for j in range(1, vis_count):
            copy3(k, j).start()
    loads[3].wait()
    loads[4].wait()
    for k in range(grid_count):
        for j in range(1, vis_count):
            copy3(k, j).wait_recv()
    sign = jnp.where(lax.broadcasted_iota(jnp.int32, (1, LANES), 1) < CONTRIB, -1.0, 1.0)
    for g in range(groups):
        straight = gathered[NBLK * g : NBLK * (g + 1)].reshape(SUB, LANES)
        turned = pltpu.roll(straight.astype(jnp.float32), CONTRIB, 1) * sign
        both = jnp.concatenate([straight, turned.astype(jnp.bfloat16)], 0)
        mixture = jnp.dot(embed[...], both, preferred_element_type=jnp.float32)
        out[:, LANES * g : LANES * (g + 1)] = (mixture * scale[...]).astype(jnp.bfloat16)
    for k in range(1, vis_count):
        copy1(k).wait_send()
    for k in range(1, grid_count):
        copy2(k).wait_send()
    for k in range(grid_count):
        for j in range(1, vis_count):
            copy3(k, j).wait_send()


def image_kernel(mixture, table, weight, out):
    result = jnp.dot(mixture[...], table[...], preferred_element_type=jnp.float32)
    out[0, 0] = result * weight[...]


def shards(grid_count, vis_count, vis_coords, vis_values, tile_index):
    groups = grid_count // NBLK
    quarter = CONTRIB // vis_count
    rows_here = FAC // vis_count
    unitary = 1.0 / math.sqrt(SUB)
    bf16, f32 = jnp.bfloat16, jnp.float32
    blocks = vis_coords.shape[1]
    visible = vis_coords.shape[3]
    partial = pl.pallas_call(
        grid_kernel,
        out_shape=jax.ShapeDtypeStruct((SUB, 2 * SUB), bf16),
        in_specs=[
            pl.BlockSpec(memory_space=pltpu.SMEM),
            pl.BlockSpec(memory_space=pltpu.VMEM),
            pl.BlockSpec(memory_space=pltpu.VMEM),
        ],
        out_specs=pl.BlockSpec(memory_space=pltpu.VMEM),
        scratch_shapes=[pltpu.VMEM((SUB, 2 * SUB), f32)],
        name="gridding",
    )(tile_index, vis_coords.reshape(blocks, 2, visible), vis_values.reshape(blocks, 2, visible))

    row_scale = taper() * (unitary / math.sqrt(CONTRIB * groups))
    row_scale = np.broadcast_to(row_scale[:, None], (FAC, LANES)).astype(np.float32)
    any_spec = pl.BlockSpec(memory_space=pl.ANY)
    dma = pltpu.SemaphoreType.DMA
    mixture = pl.pallas_call(
        functools.partial(exchange_kernel, grid_count, vis_count, unitary),
        out_shape=jax.ShapeDtypeStruct((rows_here, groups * LANES), bf16),
        in_specs=[any_spec] * 5,
        out_specs=pl.BlockSpec(memory_space=pltpu.VMEM),
        scratch_shapes=[
            pltpu.VMEM((SUB, 2 * SUB), bf16),
            pltpu.VMEM((2 * SUB, groups * 2 * LANES), bf16),
            pltpu.VMEM((SUB, 2 * SUB), bf16),
            pltpu.VMEM((rows_here, 2 * SUB), bf16),
            pltpu.VMEM((rows_here, LANES), f32),
            pltpu.VMEM((vis_count, grid_count, quarter, LANES), bf16),
            pltpu.VMEM((vis_count, grid_count, quarter, LANES), bf16),
            pltpu.VMEM((grid_count, quarter, LANES), bf16),
            pltpu.VMEM((grid_count, vis_count, quarter, LANES), bf16),
            dma((5,)),
            dma((vis_count,)),
            dma((vis_count,)),
            dma((grid_count,)),
            dma((grid_count,)),
            dma((grid_count, vis_count)),
            dma((grid_count, vis_count)),
        ],
        compiler_params=pltpu.CompilerParams(collective_id=0, has_side_effects=True),
        name="exchange",
    )(
        partial,
        jnp.asarray(column_table(groups)),
        jnp.asarray(row_table(vis_count)),
        jnp.asarray(embed_table()),
        jnp.asarray(row_scale),
    )

    halves = 2
    wide = FAC // halves
    return pl.pallas_call(
        image_kernel,
        grid=(2, halves),
        out_shape=jax.ShapeDtypeStruct((1, 2, rows_here, FAC), f32),
        in_specs=[
            pl.BlockSpec((rows_here, groups * LANES), lambda c, h: (0, 0)),
            pl.BlockSpec((groups * LANES, wide), lambda c, h: (0, c * halves + h)),
            pl.BlockSpec((1, wide), lambda c, h: (0, h)),
        ],
        out_specs=pl.BlockSpec((1, 1, rows_here, wide), lambda c, h: (0, c, 0, h)),
        name="images",
    )(
        mixture,
        jnp.asarray(output_table(groups)),
        jnp.asarray(taper()[None, :].astype(np.float32)),
    )


def solution(mesh):
    placed = (P("grid", "vis", None, None), P("grid", "vis", None, None), P("grid", "vis"))
    body = functools.partial(shards, mesh.shape["grid"], mesh.shape["vis"])
    return jax.shard_map(
        body, mesh=mesh, in_specs=placed, out_specs=P("grid", None, "vis", None), check_vma=False
    )
```

```python
import functools
import math

import jax
import jax.numpy as jnp
import ml_dtypes
import numpy as np
from jax import lax
from jax.experimental import pallas as pl
from jax.experimental.pallas import tpu as pltpu
from jax.sharding import PartitionSpec as P

SUB = 512
FAC = 1024
CONTRIB = 64
TILE = 64
NBLK = 8
LANES = 2 * CONTRIB
TAPER_SCALE = 16.0
LOADS = 4
SAVES = 4
JOINT = 4
ROOM = 24 * 2**20
MESH = pl.DeviceIdType.MESH


def phase_pair(frequencies, points, length):
    phases = (frequencies[:, None] * points[None, :]) % length
    angles = phases * (2.0 * math.pi / length)
    return np.cos(angles).astype(np.float32), np.sin(angles).astype(np.float32)


def as_bf16(array):
    return array.astype(ml_dtypes.bfloat16)


def column_table(groups):
    cos, sin = phase_pair(np.arange(SUB), np.arange(groups * CONTRIB), SUB)
    across = SUB // TILE
    table = np.zeros((across, 2, TILE, groups, 4, CONTRIB), np.float32)
    cos = cos.reshape(across, TILE, groups, CONTRIB)
    sin = sin.reshape(across, TILE, groups, CONTRIB)
    table[:, 0, :, :, 0], table[:, 1, :, :, 0] = cos, sin
    table[:, 0, :, :, 1], table[:, 1, :, :, 1] = -sin, cos
    table[:, :, :, :, 2] = -table[:, :, :, :, 1]
    table[:, :, :, :, 3] = table[:, :, :, :, 0]
    return as_bf16(table.reshape(2 * SUB, groups * 4 * CONTRIB))


def row_table(vis_count):
    quarter = CONTRIB // vis_count
    order = np.arange(SUB).reshape(NBLK, vis_count, quarter).transpose(1, 0, 2).reshape(SUB)
    cos, sin = phase_pair(order, np.arange(SUB), SUB)
    return as_bf16(np.concatenate([cos, -sin], 1))


def embed_table():
    cos, sin = phase_pair(np.arange(FAC), np.arange(SUB), FAC)
    return as_bf16(np.concatenate([cos, sin], 1))


def output_table(groups):
    cos, sin = phase_pair(np.arange(groups * CONTRIB), np.arange(FAC), FAC)
    cos = cos.reshape(groups, CONTRIB, FAC)
    sin = sin.reshape(groups, CONTRIB, FAC)
    real = np.stack([cos, -sin], 1).reshape(groups * LANES, FAC)
    imag = np.stack([sin, cos], 1).reshape(groups * LANES, FAC)
    return as_bf16(np.concatenate([real, imag], 1))


def taper():
    sines = np.sin(np.pi * (np.arange(FAC) + 0.5) / FAC)
    return 0.25 + 0.75 * sines * sines


SINE = [(-1.0) ** k * math.pi ** (2 * k) / math.factorial(2 * k + 1) for k in range(7)]


def grid_kernel(tiles, coords_hbm, values_hbm, out, coords, values, total, load_sem):
    blocks = coords.shape[0]
    chunk = blocks // LOADS

    def loads(i):
        part = pl.ds(i * chunk, chunk)
        return (
            pltpu.make_async_copy(coords_hbm.at[part], coords.at[part], load_sem.at[i, 0]),
            pltpu.make_async_copy(values_hbm.at[part], values.at[part], load_sem.at[i, 1]),
        )

    for i in range(LOADS):
        for load in loads(i):
            load.start()
    total[...] = jnp.zeros_like(total)
    lane = lax.broadcasted_iota(jnp.int32, (8, 1), 0)
    step = lane.astype(jnp.float32)
    flip = 1.0 - 2.0 * (lane % 2).astype(jnp.float32)

    def several(b, carry):
        where = coords[pl.ds(b * JOINT, JOINT)]
        count, axes, visible = where.shape
        where = where.reshape(count * axes, visible)
        nearest = jnp.floor(where + 0.5)
        where = jnp.where(where == nearest, where * (1.0 + 2.0**-23) + 1e-30, where)
        offset = where - nearest
        square = offset * offset
        wave = square * SINE[6] + SINE[5]
        for k in range(4, -1, -1):
            wave = wave * square + SINE[k]
        half = nearest * 0.5
        odd = (half - jnp.floor(half)) * 4.0 - 1.0
        wave = wave * offset * odd

        def rows(i):
            base = step - where[i : i + 1]
            fall = jnp.exp(base * base * (-1.0 / (TAPER_SCALE * TAPER_SCALE)))
            ratio = jnp.exp(base * (-16.0 / (TAPER_SCALE * TAPER_SCALE)))
            height = (flip * wave[i : i + 1]) * fall
            result = []
            for a in range(TILE // 8):
                distance = base + 8.0 * a if a else base
                near = pl.reciprocal(distance, approx=True)
                near = near * (2.0 - distance * near)
                result.append(height * near)
                height = height * ratio
            return jnp.concatenate(result, 0).astype(jnp.bfloat16)

        for i in range(count):
            along = rows(2 * i)
            down = rows(2 * i + 1).reshape(TILE // 16, 16, visible)
            data = values[b * JOINT + i]
            right = jnp.concatenate(
                [
                    (down * jnp.broadcast_to(data[c : c + 1], (16, visible)).astype(jnp.bfloat16))
                    .reshape(TILE, visible)
                    for c in range(2)
                ],
                0,
            )
            patch = lax.dot_general(
                along, right, (((1,), (1,)), ((), ())), preferred_element_type=jnp.float32
            )
            tile = tiles[0, b * JOINT + i]
            r = pl.ds(pl.multiple_of(tile // (SUB // TILE) * TILE, TILE), TILE)
            c = pl.ds(pl.multiple_of(tile % (SUB // TILE) * (2 * TILE), 2 * TILE), 2 * TILE)
            total[r, c] += patch
        return carry

    def portion(i, carry):
        for load in loads(i):
            load.wait()
        return lax.fori_loop(i * (chunk // JOINT), (i + 1) * (chunk // JOINT), several, carry)

    lax.fori_loop(0, LOADS, portion, 0)
    group = lax.broadcasted_iota(jnp.int32, (TILE, 2 * TILE), 0) // 8
    other = lax.broadcasted_iota(jnp.int32, (TILE, 2 * TILE), 1) % TILE // 8
    power = (group * group + other * other).astype(jnp.float32)
    scale = jnp.exp(power * (-64.0 / (TAPER_SCALE * TAPER_SCALE)))
    for a in range(SUB // TILE):
        for e in range(SUB // TILE):
            part = (slice(a * TILE, (a + 1) * TILE), slice(e * 2 * TILE, (e + 1) * 2 * TILE))
            out[part] = (total[part] * scale).astype(jnp.bfloat16)


def swapped(index, bits):
    result = index
    bit = 1
    while bit <= bits:
        if bits & bit:
            result = result + bit * (1 - 2 * ((index // bit) % 2))
        bit *= 2
    return result


def exchange_kernel(
    grid_count, vis_count, unitary, part_hbm, col_hbm, row_hbm, embed_hbm, scale_hbm, out,
    part, col, row, embed, scale, spectra, pieces, summed, gathered,
    load_sem, send1, recv1, send2, recv2, send3, recv3,
):
    me_g, me_v = lax.axis_index("grid"), lax.axis_index("vis")
    groups = grid_count // NBLK
    rows_here = out.shape[0]
    quarter = CONTRIB // vis_count
    peers_v = [lax.rem(me_v + k, vis_count) for k in range(vis_count)]
    peers_g = [swapped(me_g, k) for k in range(grid_count)]
    mine = pl.ds(pl.multiple_of(me_v * rows_here, rows_here), rows_here)
    loads = [
        pltpu.make_async_copy(src, dst, load_sem.at[i])
        for i, (src, dst) in enumerate(
            [(part_hbm, part), (col_hbm, col), (row_hbm, row),
             (embed_hbm.at[mine], embed), (scale_hbm.at[mine], scale)]
        )
    ]
    for load in loads:
        load.start()
    barrier = pltpu.get_barrier_semaphore()
    for k in range(grid_count - 1, 0, -1):
        pl.semaphore_signal(barrier, inc=1, device_id=(peers_g[k], me_v), device_id_type=MESH)
    for k in range(1, vis_count):
        pl.semaphore_signal(barrier, inc=1, device_id=(me_g, peers_v[k]), device_id_type=MESH)

    for load in loads[:3]:
        load.wait()
    for g in range(groups):
        image = jnp.dot(
            part[...], col[:, 2 * LANES * g : 2 * LANES * (g + 1)], preferred_element_type=jnp.float32
        )
        image = (image * unitary).astype(jnp.bfloat16)
        both = jnp.concatenate([image[:, :LANES], image[:, LANES:]], 0)
        result = jnp.dot(row[...], both, preferred_element_type=jnp.float32)
        result = (result * unitary).astype(jnp.bfloat16)
        spectra[:, NBLK * g : NBLK * (g + 1)] = result.reshape(vis_count, NBLK, quarter, LANES)

    pl.semaphore_wait(barrier, grid_count + vis_count - 2)

    def copy1(k):
        return pltpu.make_async_remote_copy(
            src_ref=spectra.at[peers_v[k]], dst_ref=pieces.at[k], send_sem=send1.at[k],
            recv_sem=recv1.at[k], device_id=(me_g, peers_v[k]), device_id_type=MESH,
        )

    def copy2(k):
        return pltpu.make_async_remote_copy(
            src_ref=summed.at[peers_g[k]], dst_ref=gathered.at[me_g, me_v], send_sem=send2.at[k],
            recv_sem=recv2.at[k], device_id=(peers_g[k], me_v), device_id_type=MESH,
        )

    def copy3(k, j):
        spot = gathered.at[peers_g[k], me_v]
        return pltpu.make_async_remote_copy(
            src_ref=spot, dst_ref=spot, send_sem=send3.at[k, j],
            recv_sem=recv3.at[k, j], device_id=(me_g, peers_v[j]), device_id_type=MESH,
        )

    for k in range(1, vis_count):
        copy1(k).start()
    whole = spectra[me_v].astype(jnp.float32)
    for k in range(1, vis_count):
        copy1(k).wait_recv()
        whole = whole + pieces[k].astype(jnp.float32)
    summed[...] = whole.astype(jnp.bfloat16)
    for k in range(grid_count - 1, 0, -1):
        copy2(k).start()
    gathered[me_g, me_v] = summed[me_g]
    for k in range(grid_count):
        if k > 0:
            copy2(k).wait_recv()
        for j in range(1, vis_count):
            copy3(k, j).start()
    loads[3].wait()
    loads[4].wait()
    for k in range(grid_count):
        for j in range(1, vis_count):
            copy3(k, j).wait_recv()
    sign = jnp.where(lax.broadcasted_iota(jnp.int32, (1, LANES), 1) < CONTRIB, -1.0, 1.0)
    for g in range(groups):
        straight = gathered[NBLK * g : NBLK * (g + 1)].reshape(SUB, LANES)
        turned = pltpu.roll(straight.astype(jnp.float32), CONTRIB, 1) * sign
        both = jnp.concatenate([straight, turned.astype(jnp.bfloat16)], 0)
        mixture = jnp.dot(embed[...], both, preferred_element_type=jnp.float32)
        out[:, LANES * g : LANES * (g + 1)] = (mixture * scale[...]).astype(jnp.bfloat16)
    for k in range(1, vis_count):
        copy1(k).wait_send()
    for k in range(1, grid_count):
        copy2(k).wait_send()
    for k in range(grid_count):
        for j in range(1, vis_count):
            copy3(k, j).wait_send()


def image_kernel(mixture, table, weight, out, image, save_sem):
    rows_here = mixture.shape[0]
    saves = []
    for c in range(2):
        for h in range(SAVES):
            part = slice(h * (rows_here // SAVES), (h + 1) * (rows_here // SAVES))
            result = jnp.dot(
                mixture[part], table[:, c * FAC : (c + 1) * FAC], preferred_element_type=jnp.float32
            )
            image[c, part] = result * weight[...]
            saves.append(
                pltpu.make_async_copy(
                    image.at[c, part], out.at[0, c, part], save_sem.at[c * SAVES + h]
                )
            )
            saves[-1].start()
    for save in saves:
        save.wait()


def shards(grid_count, vis_count, vis_coords, vis_values, tile_index):
    groups = grid_count // NBLK
    quarter = CONTRIB // vis_count
    rows_here = FAC // vis_count
    unitary = 1.0 / math.sqrt(SUB)
    bf16, f32 = jnp.bfloat16, jnp.float32
    far = pl.BlockSpec(memory_space=pltpu.HBM)
    inside = pl.BlockSpec(memory_space=pltpu.VMEM)
    dma = pltpu.SemaphoreType.DMA
    blocks = vis_coords.shape[1]
    visible = vis_coords.shape[3]
    partial = pl.pallas_call(
        grid_kernel,
        out_shape=jax.ShapeDtypeStruct((SUB, 2 * SUB), bf16),
        in_specs=[
            pl.BlockSpec(memory_space=pltpu.SMEM),
            far,
            far,
        ],
        out_specs=pl.BlockSpec(memory_space=pltpu.VMEM),
        scratch_shapes=[
            pltpu.VMEM((blocks, 2, visible), f32),
            pltpu.VMEM((blocks, 2, visible), f32),
            pltpu.VMEM((SUB, 2 * SUB), f32),
            dma((LOADS, 2)),
        ],
        name="gridding",
    )(tile_index, vis_coords.reshape(blocks, 2, visible), vis_values.reshape(blocks, 2, visible))

    row_scale = taper() * (unitary / math.sqrt(CONTRIB * groups))
    row_scale = np.broadcast_to(row_scale[:, None], (FAC, LANES)).astype(np.float32)
    mixture = pl.pallas_call(
        functools.partial(exchange_kernel, grid_count, vis_count, unitary),
        out_shape=jax.ShapeDtypeStruct((rows_here, groups * LANES), bf16),
        in_specs=[far] * 5,
        out_specs=pl.BlockSpec(memory_space=pltpu.VMEM),
        scratch_shapes=[
            pltpu.VMEM((SUB, 2 * SUB), bf16),
            pltpu.VMEM((2 * SUB, groups * 2 * LANES), bf16),
            pltpu.VMEM((SUB, 2 * SUB), bf16),
            pltpu.VMEM((rows_here, 2 * SUB), bf16),
            pltpu.VMEM((rows_here, LANES), f32),
            pltpu.VMEM((vis_count, grid_count, quarter, LANES), bf16),
            pltpu.VMEM((vis_count, grid_count, quarter, LANES), bf16),
            pltpu.VMEM((grid_count, quarter, LANES), bf16),
            pltpu.VMEM((grid_count, vis_count, quarter, LANES), bf16),
            dma((5,)),
            dma((vis_count,)),
            dma((vis_count,)),
            dma((grid_count,)),
            dma((grid_count,)),
            dma((grid_count, vis_count)),
            dma((grid_count, vis_count)),
        ],
        compiler_params=pltpu.CompilerParams(collective_id=0, has_side_effects=True),
        name="exchange",
    )(
        partial,
        jnp.asarray(column_table(groups)),
        jnp.asarray(row_table(vis_count)),
        jnp.asarray(embed_table()),
        jnp.asarray(row_scale),
    )

    return pl.pallas_call(
        image_kernel,
        out_shape=jax.ShapeDtypeStruct((1, 2, rows_here, FAC), f32),
        in_specs=[inside] * 3,
        out_specs=far,
        scratch_shapes=[pltpu.VMEM((2, rows_here, FAC), f32), dma((2 * SAVES,))],
        compiler_params=pltpu.CompilerParams(vmem_limit_bytes=ROOM),
        name="images",
    )(
        mixture,
        jnp.asarray(output_table(groups)),
        jnp.asarray(taper()[None, :].astype(np.float32)),
    )


def solution(mesh):
    placed = (P("grid", "vis", None, None), P("grid", "vis", None, None), P("grid", "vis"))
    body = functools.partial(shards, mesh.shape["grid"], mesh.shape["vis"])
    return jax.shard_map(
        body, mesh=mesh, in_specs=placed, out_specs=P("grid", None, "vis", None), check_vma=False
    )
```

```python
import functools
import math

import jax
import jax.numpy as jnp
import ml_dtypes
import numpy as np
from jax import lax
from jax.experimental import pallas as pl
from jax.experimental.pallas import tpu as pltpu
from jax.sharding import PartitionSpec as P

SUB = 512
FAC = 1024
CONTRIB = 64
TILE = 64
NBLK = 8
LANES = 2 * CONTRIB
TAPER_SCALE = 16.0
SAVES = 4
JOINT = 16
ROOM = 24 * 2**20
MESH = pl.DeviceIdType.MESH


def phase_pair(frequencies, points, length):
    phases = (frequencies[:, None] * points[None, :]) % length
    angles = phases * (2.0 * math.pi / length)
    return np.cos(angles).astype(np.float32), np.sin(angles).astype(np.float32)


def as_bf16(array):
    return array.astype(ml_dtypes.bfloat16)


def column_table(groups):
    cos, sin = phase_pair(np.arange(SUB), np.arange(groups * CONTRIB), SUB)
    across = SUB // TILE
    table = np.zeros((across, 2, TILE, groups, 4, CONTRIB), np.float32)
    cos = cos.reshape(across, TILE, groups, CONTRIB)
    sin = sin.reshape(across, TILE, groups, CONTRIB)
    table[:, 0, :, :, 0], table[:, 1, :, :, 0] = cos, sin
    table[:, 0, :, :, 1], table[:, 1, :, :, 1] = -sin, cos
    table[:, :, :, :, 2] = -table[:, :, :, :, 1]
    table[:, :, :, :, 3] = table[:, :, :, :, 0]
    return as_bf16(table.reshape(2 * SUB, groups * 4 * CONTRIB))


def row_table(vis_count):
    quarter = CONTRIB // vis_count
    order = np.arange(SUB).reshape(NBLK, vis_count, quarter).transpose(1, 0, 2).reshape(SUB)
    cos, sin = phase_pair(order, np.arange(SUB), SUB)
    return as_bf16(np.concatenate([cos, -sin], 1))


def embed_table():
    cos, sin = phase_pair(np.arange(FAC), np.arange(SUB), FAC)
    return as_bf16(np.concatenate([cos, sin], 1))


def output_table(groups):
    cos, sin = phase_pair(np.arange(groups * CONTRIB), np.arange(FAC), FAC)
    cos = cos.reshape(groups, CONTRIB, FAC)
    sin = sin.reshape(groups, CONTRIB, FAC)
    real = np.stack([cos, -sin], 1).reshape(groups * LANES, FAC)
    imag = np.stack([sin, cos], 1).reshape(groups * LANES, FAC)
    return as_bf16(np.concatenate([real, imag], 1))


def taper():
    sines = np.sin(np.pi * (np.arange(FAC) + 0.5) / FAC)
    return 0.25 + 0.75 * sines * sines


SINE = [(-1.0) ** k * math.pi ** (2 * k) / math.factorial(2 * k + 1) for k in range(7)]


def grid_kernel(
    tiles_hbm, coords_hbm, values_hbm, out, tiles, coords, values, total, tile_sem, load_sem
):
    blocks = coords.shape[0]

    def loads(i):
        part = pl.ds(i * JOINT, JOINT)
        return (
            pltpu.make_async_copy(coords_hbm.at[part], coords.at[part], load_sem.at[i, 0]),
            pltpu.make_async_copy(values_hbm.at[part], values.at[part], load_sem.at[i, 1]),
        )

    for i in range(blocks // JOINT):
        for load in loads(i):
            load.start()
        if i == 0:
            tile_load = pltpu.make_async_copy(tiles_hbm, tiles, tile_sem)
            tile_load.start()
    total[...] = jnp.zeros_like(total)
    lane = lax.broadcasted_iota(jnp.int32, (8, 1), 0)
    step = lane.astype(jnp.float32)
    flip = 1.0 - 2.0 * (lane % 2).astype(jnp.float32)

    def several(b, carry):
        for load in loads(b):
            load.wait()
        where = coords[pl.ds(b * JOINT, JOINT)]
        count, axes, visible = where.shape
        where = where.reshape(count * axes, visible)
        nearest = jnp.floor(where + 0.5)
        where = jnp.where(where == nearest, where * (1.0 + 2.0**-23) + 1e-30, where)
        offset = where - nearest
        square = offset * offset
        wave = square * SINE[6] + SINE[5]
        for k in range(4, -1, -1):
            wave = wave * square + SINE[k]
        half = nearest * 0.5
        odd = (half - jnp.floor(half)) * 4.0 - 1.0
        wave = wave * offset * odd

        def rows(i):
            base = step - where[i : i + 1]
            fall = jnp.exp(base * base * (-1.0 / (TAPER_SCALE * TAPER_SCALE)))
            ratio = jnp.exp(base * (-16.0 / (TAPER_SCALE * TAPER_SCALE)))
            height = (flip * wave[i : i + 1]) * fall
            result = []
            for a in range(TILE // 8):
                distance = base + 8.0 * a if a else base
                result.append(height / distance)
                height = height * ratio
            return jnp.concatenate(result, 0).astype(jnp.bfloat16)

        for i in range(count):
            along = rows(2 * i)
            down = rows(2 * i + 1).reshape(TILE // 16, 16, visible)
            data = values[b * JOINT + i]
            right = jnp.concatenate(
                [
                    (down * jnp.broadcast_to(data[c : c + 1], (16, visible)).astype(jnp.bfloat16))
                    .reshape(TILE, visible)
                    for c in range(2)
                ],
                0,
            )
            patch = lax.dot_general(
                along, right, (((1,), (1,)), ((), ())), preferred_element_type=jnp.float32
            )
            tile = tiles[0, b * JOINT + i]
            r = pl.ds(pl.multiple_of(tile // (SUB // TILE) * TILE, TILE), TILE)
            c = pl.ds(pl.multiple_of(tile % (SUB // TILE) * (2 * TILE), 2 * TILE), 2 * TILE)
            total[r, c] += patch
        return carry

    tile_load.wait()
    lax.fori_loop(0, blocks // JOINT, several, 0)
    group = lax.broadcasted_iota(jnp.int32, (TILE, 2 * TILE), 0) // 8
    other = lax.broadcasted_iota(jnp.int32, (TILE, 2 * TILE), 1) % TILE // 8
    power = (group * group + other * other).astype(jnp.float32)
    scale = jnp.exp(power * (-64.0 / (TAPER_SCALE * TAPER_SCALE)))
    for a in range(SUB // TILE):
        for e in range(SUB // TILE):
            part = (slice(a * TILE, (a + 1) * TILE), slice(e * 2 * TILE, (e + 1) * 2 * TILE))
            out[part] = (total[part] * scale).astype(jnp.bfloat16)


def swapped(index, bits):
    result = index
    bit = 1
    while bit <= bits:
        if bits & bit:
            result = result + bit * (1 - 2 * ((index // bit) % 2))
        bit *= 2
    return result


def exchange_kernel(
    grid_count, vis_count, unitary, part, col, row, embed, scale, out,
    spectra, pieces, summed, gathered,
    send1, recv1, send2, recv2, send3, recv3,
):
    me_g, me_v = lax.axis_index("grid"), lax.axis_index("vis")
    groups = grid_count // NBLK
    rows_here = out.shape[0]
    quarter = CONTRIB // vis_count
    peers_v = [lax.rem(me_v + k, vis_count) for k in range(vis_count)]
    peers_g = [swapped(me_g, k) for k in range(grid_count)]
    mine = pl.ds(pl.multiple_of(me_v * rows_here, rows_here), rows_here)
    barrier = pltpu.get_barrier_semaphore()
    for k in range(grid_count - 1, 0, -1):
        pl.semaphore_signal(barrier, inc=1, device_id=(peers_g[k], me_v), device_id_type=MESH)
    for k in range(1, vis_count):
        pl.semaphore_signal(barrier, inc=1, device_id=(me_g, peers_v[k]), device_id_type=MESH)

    for g in range(groups):
        image = jnp.dot(
            part[...], col[:, 2 * LANES * g : 2 * LANES * (g + 1)], preferred_element_type=jnp.float32
        )
        image = (image * unitary).astype(jnp.bfloat16)
        both = jnp.concatenate([image[:, :LANES], image[:, LANES:]], 0)
        result = jnp.dot(row[...], both, preferred_element_type=jnp.float32)
        result = (result * unitary).astype(jnp.bfloat16)
        spectra[:, NBLK * g : NBLK * (g + 1)] = result.reshape(vis_count, NBLK, quarter, LANES)

    pl.semaphore_wait(barrier, grid_count + vis_count - 2)

    def copy1(k):
        return pltpu.make_async_remote_copy(
            src_ref=spectra.at[peers_v[k]], dst_ref=pieces.at[k], send_sem=send1.at[k],
            recv_sem=recv1.at[k], device_id=(me_g, peers_v[k]), device_id_type=MESH,
        )

    def copy2(k):
        return pltpu.make_async_remote_copy(
            src_ref=summed.at[peers_g[k]], dst_ref=gathered.at[me_g, me_v], send_sem=send2.at[k],
            recv_sem=recv2.at[k], device_id=(peers_g[k], me_v), device_id_type=MESH,
        )

    def copy3(k, j):
        spot = gathered.at[peers_g[k], me_v]
        return pltpu.make_async_remote_copy(
            src_ref=spot, dst_ref=spot, send_sem=send3.at[k, j],
            recv_sem=recv3.at[k, j], device_id=(me_g, peers_v[j]), device_id_type=MESH,
        )

    for k in range(1, vis_count):
        copy1(k).start()
    whole = spectra[me_v].astype(jnp.float32)
    for k in range(1, vis_count):
        copy1(k).wait_recv()
        whole = whole + pieces[k].astype(jnp.float32)
    summed[...] = whole.astype(jnp.bfloat16)
    for k in range(grid_count - 1, 0, -1):
        copy2(k).start()
    gathered[me_g, me_v] = summed[me_g]
    for k in range(grid_count):
        if k > 0:
            copy2(k).wait_recv()
        for j in range(1, vis_count):
            copy3(k, j).start()
    for k in range(grid_count):
        for j in range(1, vis_count):
            copy3(k, j).wait_recv()
    sign = jnp.where(lax.broadcasted_iota(jnp.int32, (1, LANES), 1) < CONTRIB, -1.0, 1.0)
    for g in range(groups):
        straight = gathered[NBLK * g : NBLK * (g + 1)].reshape(SUB, LANES)
        turned = pltpu.roll(straight.astype(jnp.float32), CONTRIB, 1) * sign
        both = jnp.concatenate([straight, turned.astype(jnp.bfloat16)], 0)
        mixture = jnp.dot(embed[mine], both, preferred_element_type=jnp.float32)
        out[:, LANES * g : LANES * (g + 1)] = (mixture * scale[mine]).astype(jnp.bfloat16)
    for k in range(1, vis_count):
        copy1(k).wait_send()
    for k in range(1, grid_count):
        copy2(k).wait_send()
    for k in range(grid_count):
        for j in range(1, vis_count):
            copy3(k, j).wait_send()


def image_kernel(mixture, table, weight, out, image, save_sem):
    rows_here = mixture.shape[0]
    saves = []
    for c in range(2):
        for h in range(SAVES):
            part = slice(h * (rows_here // SAVES), (h + 1) * (rows_here // SAVES))
            result = jnp.dot(
                mixture[part], table[:, c * FAC : (c + 1) * FAC], preferred_element_type=jnp.float32
            )
            image[c, part] = result * weight[...]
            saves.append(
                pltpu.make_async_copy(
                    image.at[c, part], out.at[0, c, part], save_sem.at[c * SAVES + h]
                )
            )
            saves[-1].start()
    for save in saves:
        save.wait()


def shards(grid_count, vis_count, vis_coords, vis_values, tile_index):
    groups = grid_count // NBLK
    quarter = CONTRIB // vis_count
    rows_here = FAC // vis_count
    unitary = 1.0 / math.sqrt(SUB)
    bf16, f32 = jnp.bfloat16, jnp.float32
    far = pl.BlockSpec(memory_space=pltpu.HBM)
    inside = pl.BlockSpec(memory_space=pltpu.VMEM)
    dma = pltpu.SemaphoreType.DMA
    blocks = vis_coords.shape[1]
    visible = vis_coords.shape[3]
    partial = pl.pallas_call(
        grid_kernel,
        out_shape=jax.ShapeDtypeStruct((SUB, 2 * SUB), bf16),
        in_specs=[
            far,
            far,
            far,
        ],
        out_specs=pl.BlockSpec(memory_space=pltpu.VMEM),
        scratch_shapes=[
            pltpu.SMEM((1, blocks), jnp.int32),
            pltpu.VMEM((blocks, 2, visible), f32),
            pltpu.VMEM((blocks, 2, visible), f32),
            pltpu.VMEM((SUB, 2 * SUB), f32),
            dma,
            dma((blocks // JOINT, 2)),
        ],
        compiler_params=pltpu.CompilerParams(vmem_limit_bytes=ROOM),
        cost_estimate=pl.CostEstimate(flops=10**10, bytes_accessed=10**6, transcendentals=10**6),
        name="gridding",
    )(
        pltpu.with_memory_space_constraint(tile_index, pltpu.HBM),
        pltpu.with_memory_space_constraint(vis_coords.reshape(blocks, 2, visible), pltpu.HBM),
        pltpu.with_memory_space_constraint(vis_values.reshape(blocks, 2, visible), pltpu.HBM),
    )

    row_scale = taper() * (unitary / math.sqrt(CONTRIB * groups))
    row_scale = np.broadcast_to(row_scale[:, None], (FAC, LANES)).astype(np.float32)
    mixture = pl.pallas_call(
        functools.partial(exchange_kernel, grid_count, vis_count, unitary),
        out_shape=jax.ShapeDtypeStruct((rows_here, groups * LANES), bf16),
        in_specs=[inside] * 5,
        out_specs=pl.BlockSpec(memory_space=pltpu.VMEM),
        scratch_shapes=[
            pltpu.VMEM((vis_count, grid_count, quarter, LANES), bf16),
            pltpu.VMEM((vis_count, grid_count, quarter, LANES), bf16),
            pltpu.VMEM((grid_count, quarter, LANES), bf16),
            pltpu.VMEM((grid_count, vis_count, quarter, LANES), bf16),
            dma((vis_count,)),
            dma((vis_count,)),
            dma((grid_count,)),
            dma((grid_count,)),
            dma((grid_count, vis_count)),
            dma((grid_count, vis_count)),
        ],
        compiler_params=pltpu.CompilerParams(
            collective_id=0, has_side_effects=True, vmem_limit_bytes=ROOM
        ),
        cost_estimate=pl.CostEstimate(flops=10**10, bytes_accessed=10**6, transcendentals=0),
        name="exchange",
    )(
        partial,
        jnp.asarray(column_table(groups)),
        jnp.asarray(row_table(vis_count)),
        jnp.asarray(embed_table()),
        jnp.asarray(row_scale),
    )

    return pl.pallas_call(
        image_kernel,
        out_shape=jax.ShapeDtypeStruct((1, 2, rows_here, FAC), f32),
        in_specs=[inside] * 3,
        out_specs=far,
        scratch_shapes=[pltpu.VMEM((2, rows_here, FAC), f32), dma((2 * SAVES,))],
        compiler_params=pltpu.CompilerParams(vmem_limit_bytes=ROOM),
        name="images",
    )(
        mixture,
        jnp.asarray(output_table(groups)),
        jnp.asarray(taper()[None, :].astype(np.float32)),
    )


def solution(mesh):
    placed = (P("grid", "vis", None, None), P("grid", "vis", None, None), P("grid", "vis"))
    body = functools.partial(shards, mesh.shape["grid"], mesh.shape["vis"])
    return jax.shard_map(
        body, mesh=mesh, in_specs=placed, out_specs=P("grid", None, "vis", None), check_vma=False
    )
```

```python
import functools
import math

import jax
import jax.numpy as jnp
import ml_dtypes
import numpy as np
from jax import lax
from jax.experimental import pallas as pl
from jax.experimental.pallas import tpu as pltpu
from jax.sharding import PartitionSpec as P

SUB = 512
FAC = 1024
CONTRIB = 64
TILE = 64
NBLK = 8
LANES = 2 * CONTRIB
TAPER_SCALE = 16.0
SAVES = 4
JOINT = 16
ROOM = 24 * 2**20
MESH = pl.DeviceIdType.MESH


def phase_pair(frequencies, points, length):
    phases = (frequencies[:, None] * points[None, :]) % length
    angles = phases * (2.0 * math.pi / length)
    return np.cos(angles).astype(np.float32), np.sin(angles).astype(np.float32)


def as_bf16(array):
    return array.astype(ml_dtypes.bfloat16)


def column_table(groups):
    cos, sin = phase_pair(np.arange(SUB), np.arange(groups * CONTRIB), SUB)
    across = SUB // TILE
    table = np.zeros((across, 2, TILE, groups, 4, CONTRIB), np.float32)
    cos = cos.reshape(across, TILE, groups, CONTRIB)
    sin = sin.reshape(across, TILE, groups, CONTRIB)
    table[:, 0, :, :, 0], table[:, 1, :, :, 0] = cos, sin
    table[:, 0, :, :, 1], table[:, 1, :, :, 1] = -sin, cos
    table[:, :, :, :, 2] = -table[:, :, :, :, 1]
    table[:, :, :, :, 3] = table[:, :, :, :, 0]
    return as_bf16(table.reshape(2 * SUB, groups * 4 * CONTRIB))


def row_table(vis_count):
    quarter = CONTRIB // vis_count
    order = np.arange(SUB).reshape(NBLK, vis_count, quarter).transpose(1, 0, 2).reshape(SUB)
    cos, sin = phase_pair(order, np.arange(SUB), SUB)
    return as_bf16(np.concatenate([cos, -sin], 1))


def embed_table():
    cos, sin = phase_pair(np.arange(FAC), np.arange(SUB), FAC)
    return as_bf16(np.concatenate([cos, sin], 1))


def output_table(groups):
    cos, sin = phase_pair(np.arange(groups * CONTRIB), np.arange(FAC), FAC)
    cos = cos.reshape(groups, CONTRIB, FAC)
    sin = sin.reshape(groups, CONTRIB, FAC)
    real = np.stack([cos, -sin], 1).reshape(groups * LANES, FAC)
    imag = np.stack([sin, cos], 1).reshape(groups * LANES, FAC)
    return as_bf16(np.concatenate([real, imag], 1))


def taper():
    sines = np.sin(np.pi * (np.arange(FAC) + 0.5) / FAC)
    return 0.25 + 0.75 * sines * sines


SINE = [(-1.0) ** k * math.pi ** (2 * k) / math.factorial(2 * k + 1) for k in range(7)]


def grid_kernel(
    tiles_hbm, coords_hbm, values_hbm, total, tiles, coords, values, tile_sem, load_sem
):
    blocks = coords.shape[0]

    def loads(i):
        part = pl.ds(i * JOINT, JOINT)
        return (
            pltpu.make_async_copy(coords_hbm.at[part], coords.at[part], load_sem.at[i, 0]),
            pltpu.make_async_copy(values_hbm.at[part], values.at[part], load_sem.at[i, 1]),
        )

    for i in range(blocks // JOINT):
        for load in loads(i):
            load.start()
        if i == 0:
            tile_load = pltpu.make_async_copy(tiles_hbm, tiles, tile_sem)
            tile_load.start()
    total[...] = jnp.zeros_like(total)
    lane = lax.broadcasted_iota(jnp.int32, (8, 1), 0)
    step = lane.astype(jnp.float32)
    flip = 1.0 - 2.0 * (lane % 2).astype(jnp.float32)

    def several(b, carry):
        for load in loads(b):
            load.wait()
        where = coords[pl.ds(b * JOINT, JOINT)]
        count, axes, visible = where.shape
        where = where.reshape(count * axes, visible)
        nearest = jnp.floor(where + 0.5)
        where = jnp.where(where == nearest, where * (1.0 + 2.0**-23) + 1e-30, where)
        offset = where - nearest
        square = offset * offset
        wave = square * SINE[6] + SINE[5]
        for k in range(4, -1, -1):
            wave = wave * square + SINE[k]
        half = nearest * 0.5
        odd = (half - jnp.floor(half)) * 4.0 - 1.0
        wave = wave * offset * odd

        def rows(i):
            base = step - where[i : i + 1]
            fall = jnp.exp(base * base * (-1.0 / (TAPER_SCALE * TAPER_SCALE)))
            ratio = jnp.exp(base * (-16.0 / (TAPER_SCALE * TAPER_SCALE)))
            height = (flip * wave[i : i + 1]) * fall
            result = []
            for a in range(TILE // 8):
                distance = base + 8.0 * a if a else base
                result.append(height / distance)
                height = height * ratio
            return jnp.concatenate(result, 0).astype(jnp.bfloat16)

        for i in range(count):
            along = rows(2 * i)
            down = rows(2 * i + 1).reshape(TILE // 16, 16, visible)
            data = values[b * JOINT + i]
            right = jnp.concatenate(
                [
                    (down * jnp.broadcast_to(data[c : c + 1], (16, visible)).astype(jnp.bfloat16))
                    .reshape(TILE, visible)
                    for c in range(2)
                ],
                0,
            )
            patch = lax.dot_general(
                along, right, (((1,), (1,)), ((), ())), preferred_element_type=jnp.float32
            )
            tile = tiles[0, b * JOINT + i]
            r = pl.ds(pl.multiple_of(tile // (SUB // TILE) * TILE, TILE), TILE)
            c = pl.ds(pl.multiple_of(tile % (SUB // TILE) * (2 * TILE), 2 * TILE), 2 * TILE)
            total[r, c] += patch
        return carry

    tile_load.wait()
    lax.fori_loop(0, blocks // JOINT, several, 0)


def swapped(index, bits):
    result = index
    bit = 1
    while bit <= bits:
        if bits & bit:
            result = result + bit * (1 - 2 * ((index // bit) % 2))
        bit *= 2
    return result


def exchange_kernel(
    grid_count, vis_count, unitary, total, col, row, embed, scale, out,
    part, spectra, pieces, summed, gathered,
    send1, recv1, send2, recv2, send3, recv3,
):
    me_g, me_v = lax.axis_index("grid"), lax.axis_index("vis")
    groups = grid_count // NBLK
    rows_here = out.shape[0]
    quarter = CONTRIB // vis_count
    peers_v = [lax.rem(me_v + k, vis_count) for k in range(vis_count)]
    peers_g = [swapped(me_g, k) for k in range(grid_count)]
    mine = pl.ds(pl.multiple_of(me_v * rows_here, rows_here), rows_here)
    barrier = pltpu.get_barrier_semaphore()
    for k in range(grid_count - 1, 0, -1):
        pl.semaphore_signal(barrier, inc=1, device_id=(peers_g[k], me_v), device_id_type=MESH)
    for k in range(1, vis_count):
        pl.semaphore_signal(barrier, inc=1, device_id=(me_g, peers_v[k]), device_id_type=MESH)

    group = lax.broadcasted_iota(jnp.int32, (TILE, 2 * TILE), 0) // 8
    other = lax.broadcasted_iota(jnp.int32, (TILE, 2 * TILE), 1) % TILE // 8
    power = (group * group + other * other).astype(jnp.float32)
    fall = jnp.exp(power * (-64.0 / (TAPER_SCALE * TAPER_SCALE)))
    for a in range(SUB // TILE):
        for e in range(SUB // TILE):
            spot = (slice(a * TILE, (a + 1) * TILE), slice(e * 2 * TILE, (e + 1) * 2 * TILE))
            part[spot] = (total[spot] * fall).astype(jnp.bfloat16)
    for g in range(groups):
        image = jnp.dot(
            part[...], col[:, 2 * LANES * g : 2 * LANES * (g + 1)], preferred_element_type=jnp.float32
        )
        image = (image * unitary).astype(jnp.bfloat16)
        both = jnp.concatenate([image[:, :LANES], image[:, LANES:]], 0)
        result = jnp.dot(row[...], both, preferred_element_type=jnp.float32)
        result = (result * unitary).astype(jnp.bfloat16)
        spectra[:, NBLK * g : NBLK * (g + 1)] = result.reshape(vis_count, NBLK, quarter, LANES)

    pl.semaphore_wait(barrier, grid_count + vis_count - 2)

    half = grid_count // 2
    high = me_g // half
    spots = [pl.ds((1 - high) * half, half), pl.ds(high * half, half)]

    def copy1(h, k):
        return pltpu.make_async_remote_copy(
            src_ref=spectra.at[peers_v[k], spots[h]], dst_ref=pieces.at[k, spots[h]],
            send_sem=send1.at[h, k], recv_sem=recv1.at[h, k], device_id=(me_g, peers_v[k]), device_id_type=MESH,
        )

    def copy2(k):
        return pltpu.make_async_remote_copy(
            src_ref=summed.at[peers_g[k]], dst_ref=gathered.at[me_g, me_v], send_sem=send2.at[k],
            recv_sem=recv2.at[k], device_id=(peers_g[k], me_v), device_id_type=MESH,
        )

    def copy3(k, j):
        spot = gathered.at[peers_g[k], me_v]
        return pltpu.make_async_remote_copy(
            src_ref=spot, dst_ref=spot, send_sem=send3.at[k, j],
            recv_sem=recv3.at[k, j], device_id=(me_g, peers_v[j]), device_id_type=MESH,
        )

    for h in range(2):
        for k in range(1, vis_count):
            copy1(h, k).start()
    for h in range(2):
        whole = spectra[me_v, spots[h]].astype(jnp.float32)
        for k in range(1, vis_count):
            copy1(h, k).wait_recv()
            whole = whole + pieces[k, spots[h]].astype(jnp.float32)
        summed[spots[h]] = whole.astype(jnp.bfloat16)
        for k in range(grid_count - 1, half - 1, -1) if h == 0 else range(half - 1, 0, -1):
            copy2(k).start()
    gathered[me_g, me_v] = summed[me_g]
    for k in range(grid_count):
        if k > 0:
            copy2(k).wait_recv()
        for j in range(1, vis_count):
            copy3(k, j).start()
    for k in range(grid_count):
        for j in range(1, vis_count):
            copy3(k, j).wait_recv()
    sign = jnp.where(lax.broadcasted_iota(jnp.int32, (1, LANES), 1) < CONTRIB, -1.0, 1.0)
    for g in range(groups):
        straight = gathered[NBLK * g : NBLK * (g + 1)].reshape(SUB, LANES)
        turned = pltpu.roll(straight.astype(jnp.float32), CONTRIB, 1) * sign
        both = jnp.concatenate([straight, turned.astype(jnp.bfloat16)], 0)
        mixture = jnp.dot(embed[mine], both, preferred_element_type=jnp.float32)
        out[:, LANES * g : LANES * (g + 1)] = (mixture * scale[mine]).astype(jnp.bfloat16)
    for h in range(2):
        for k in range(1, vis_count):
            copy1(h, k).wait_send()
    for k in range(1, grid_count):
        copy2(k).wait_send()
    for k in range(grid_count):
        for j in range(1, vis_count):
            copy3(k, j).wait_send()


def image_kernel(mixture, table, weight, out, image, save_sem):
    rows_here = mixture.shape[0]
    saves = []
    for c in range(2):
        for h in range(SAVES):
            part = slice(h * (rows_here // SAVES), (h + 1) * (rows_here // SAVES))
            result = jnp.dot(
                mixture[part], table[:, c * FAC : (c + 1) * FAC], preferred_element_type=jnp.float32
            )
            image[c, part] = result * weight[...]
            saves.append(
                pltpu.make_async_copy(
                    image.at[c, part], out.at[0, c, part], save_sem.at[c * SAVES + h]
                )
            )
            saves[-1].start()
    for save in saves:
        save.wait()


def shards(grid_count, vis_count, vis_coords, vis_values, tile_index):
    groups = grid_count // NBLK
    quarter = CONTRIB // vis_count
    rows_here = FAC // vis_count
    unitary = 1.0 / math.sqrt(SUB)
    bf16, f32 = jnp.bfloat16, jnp.float32
    far = pl.BlockSpec(memory_space=pltpu.HBM)
    inside = pl.BlockSpec(memory_space=pltpu.VMEM)
    dma = pltpu.SemaphoreType.DMA
    blocks = vis_coords.shape[1]
    visible = vis_coords.shape[3]
    partial = pl.pallas_call(
        grid_kernel,
        out_shape=jax.ShapeDtypeStruct((SUB, 2 * SUB), f32),
        in_specs=[
            far,
            far,
            far,
        ],
        out_specs=pl.BlockSpec(memory_space=pltpu.VMEM),
        scratch_shapes=[
            pltpu.SMEM((1, blocks), jnp.int32),
            pltpu.VMEM((blocks, 2, visible), f32),
            pltpu.VMEM((blocks, 2, visible), f32),
            dma,
            dma((blocks // JOINT, 2)),
        ],
        compiler_params=pltpu.CompilerParams(vmem_limit_bytes=ROOM),
        cost_estimate=pl.CostEstimate(flops=10**10, bytes_accessed=10**6, transcendentals=10**6),
        name="gridding",
    )(
        pltpu.with_memory_space_constraint(tile_index, pltpu.HBM),
        pltpu.with_memory_space_constraint(vis_coords.reshape(blocks, 2, visible), pltpu.HBM),
        pltpu.with_memory_space_constraint(vis_values.reshape(blocks, 2, visible), pltpu.HBM),
    )

    row_scale = taper() * (unitary / math.sqrt(CONTRIB * groups))
    row_scale = np.broadcast_to(row_scale[:, None], (FAC, LANES)).astype(np.float32)
    mixture = pl.pallas_call(
        functools.partial(exchange_kernel, grid_count, vis_count, unitary),
        out_shape=jax.ShapeDtypeStruct((rows_here, groups * LANES), bf16),
        in_specs=[inside] * 5,
        out_specs=pl.BlockSpec(memory_space=pltpu.VMEM),
        scratch_shapes=[
            pltpu.VMEM((SUB, 2 * SUB), bf16),
            pltpu.VMEM((vis_count, grid_count, quarter, LANES), bf16),
            pltpu.VMEM((vis_count, grid_count, quarter, LANES), bf16),
            pltpu.VMEM((grid_count, quarter, LANES), bf16),
            pltpu.VMEM((grid_count, vis_count, quarter, LANES), bf16),
            dma((2, vis_count)),
            dma((2, vis_count)),
            dma((grid_count,)),
            dma((grid_count,)),
            dma((grid_count, vis_count)),
            dma((grid_count, vis_count)),
        ],
        compiler_params=pltpu.CompilerParams(
            collective_id=0, has_side_effects=True, vmem_limit_bytes=ROOM
        ),
        cost_estimate=pl.CostEstimate(flops=10**10, bytes_accessed=10**6, transcendentals=0),
        name="exchange",
    )(
        partial,
        jnp.asarray(column_table(groups)),
        jnp.asarray(row_table(vis_count)),
        jnp.asarray(embed_table()),
        jnp.asarray(row_scale),
    )

    return pl.pallas_call(
        image_kernel,
        out_shape=jax.ShapeDtypeStruct((1, 2, rows_here, FAC), f32),
        in_specs=[inside] * 3,
        out_specs=far,
        scratch_shapes=[pltpu.VMEM((2, rows_here, FAC), f32), dma((2 * SAVES,))],
        compiler_params=pltpu.CompilerParams(vmem_limit_bytes=ROOM),
        name="images",
    )(
        mixture,
        jnp.asarray(output_table(groups)),
        jnp.asarray(taper()[None, :].astype(np.float32)),
    )


def solution(mesh):
    placed = (P("grid", "vis", None, None), P("grid", "vis", None, None), P("grid", "vis"))
    body = functools.partial(shards, mesh.shape["grid"], mesh.shape["vis"])
    return jax.shard_map(
        body, mesh=mesh, in_specs=placed, out_specs=P("grid", None, "vis", None), check_vma=False
    )
```

```python
import functools
import math

import jax
import jax.numpy as jnp
import ml_dtypes
import numpy as np
from jax import lax
from jax.experimental import pallas as pl
from jax.experimental.pallas import tpu as pltpu
from jax.sharding import PartitionSpec as P

SUB = 512
FAC = 1024
CONTRIB = 64
TILE = 64
NBLK = 8
LANES = 2 * CONTRIB
TAPER_SCALE = 16.0
SAVES = 4
JOINT = 32
PIECES = 4
ROOM = 24 * 2**20
MESH = pl.DeviceIdType.MESH


def phase_pair(frequencies, points, length):
    phases = (frequencies[:, None] * points[None, :]) % length
    angles = phases * (2.0 * math.pi / length)
    return np.cos(angles).astype(np.float32), np.sin(angles).astype(np.float32)


def as_bf16(array):
    return array.astype(ml_dtypes.bfloat16)


def column_table(groups):
    cos, sin = phase_pair(np.arange(SUB), np.arange(groups * CONTRIB), SUB)
    across = SUB // TILE
    table = np.zeros((across, 2, TILE, groups, 4, CONTRIB), np.float32)
    cos = cos.reshape(across, TILE, groups, CONTRIB)
    sin = sin.reshape(across, TILE, groups, CONTRIB)
    table[:, 0, :, :, 0], table[:, 1, :, :, 0] = cos, sin
    table[:, 0, :, :, 1], table[:, 1, :, :, 1] = -sin, cos
    table[:, :, :, :, 2] = -table[:, :, :, :, 1]
    table[:, :, :, :, 3] = table[:, :, :, :, 0]
    return as_bf16(table.reshape(2 * SUB, groups * 4 * CONTRIB))


def row_table(vis_count):
    quarter = CONTRIB // vis_count
    order = np.arange(SUB).reshape(NBLK, vis_count, quarter).transpose(1, 0, 2).reshape(SUB)
    cos, sin = phase_pair(order, np.arange(SUB), SUB)
    return as_bf16(np.concatenate([cos, -sin], 1))


def embed_table():
    cos, sin = phase_pair(np.arange(FAC), np.arange(SUB), FAC)
    return as_bf16(np.concatenate([cos, sin], 1))


def output_table(groups):
    cos, sin = phase_pair(np.arange(groups * CONTRIB), np.arange(FAC), FAC)
    cos = cos.reshape(groups, CONTRIB, FAC)
    sin = sin.reshape(groups, CONTRIB, FAC)
    real = np.stack([cos, -sin], 1).reshape(groups * LANES, FAC)
    imag = np.stack([sin, cos], 1).reshape(groups * LANES, FAC)
    return as_bf16(np.concatenate([real, imag], 1))


def taper():
    sines = np.sin(np.pi * (np.arange(FAC) + 0.5) / FAC)
    return 0.25 + 0.75 * sines * sines


SINE = [(-1.0) ** k * math.pi ** (2 * k) / math.factorial(2 * k + 1) for k in range(7)]


def grid_kernel(
    tiles_hbm, coords_hbm, values_hbm, total, tiles, coords, values, tile_sem, load_sem
):
    blocks = coords.shape[0]

    def loads(i):
        part = pl.ds(i * JOINT, JOINT)
        return (
            pltpu.make_async_copy(coords_hbm.at[part], coords.at[part], load_sem.at[i, 0]),
            pltpu.make_async_copy(values_hbm.at[part], values.at[part], load_sem.at[i, 1]),
        )

    for i in range(blocks // JOINT):
        for load in loads(i):
            load.start()
        if i == 0:
            tile_load = pltpu.make_async_copy(tiles_hbm, tiles, tile_sem)
            tile_load.start()
    total[...] = jnp.zeros_like(total)
    lane = lax.broadcasted_iota(jnp.int32, (8, 1), 0)
    step = lane.astype(jnp.float32)
    flip = 1.0 - 2.0 * (lane % 2).astype(jnp.float32)
    lean = jnp.exp(step * (-16.0 / (TAPER_SCALE * TAPER_SCALE)))

    def several(b, carry):
        for load in loads(b):
            load.wait()
        where = coords[pl.ds(b * JOINT, JOINT)]
        count, axes, visible = where.shape
        where = where.reshape(count * axes, visible)
        nearest = jnp.floor(where + 0.5)
        where = jnp.where(where == nearest, where * (1.0 + 2.0**-23) + 1e-30, where)
        offset = where - nearest
        square = offset * offset
        wave = square * SINE[6] + SINE[5]
        for k in range(4, -1, -1):
            wave = wave * square + SINE[k]
        half = nearest * 0.5
        odd = (half - jnp.floor(half)) * 4.0 - 1.0
        wave = wave * offset * odd
        growth = jnp.exp(where * (16.0 / (TAPER_SCALE * TAPER_SCALE)))

        def rows(i):
            base = step - where[i : i + 1]
            fall = jnp.exp(base * base * (-1.0 / (TAPER_SCALE * TAPER_SCALE)))
            ratio = lean * growth[i : i + 1]
            height = (flip * wave[i : i + 1]) * fall
            result = []
            for a in range(TILE // 8):
                distance = base + 8.0 * a if a else base
                result.append(height / distance)
                height = height * ratio
            return jnp.concatenate(result, 0).astype(jnp.bfloat16)

        for i in range(count):
            along = rows(2 * i)
            down = rows(2 * i + 1).reshape(TILE // 16, 16, visible)
            data = values[b * JOINT + i]
            right = jnp.concatenate(
                [
                    (down * jnp.broadcast_to(data[c : c + 1], (16, visible)).astype(jnp.bfloat16))
                    .reshape(TILE, visible)
                    for c in range(2)
                ],
                0,
            )
            patch = lax.dot_general(
                along, right, (((1,), (1,)), ((), ())), preferred_element_type=jnp.float32
            )
            tile = tiles[0, b * JOINT + i]
            r = pl.ds(pl.multiple_of(tile // (SUB // TILE) * TILE, TILE), TILE)
            c = pl.ds(pl.multiple_of(tile % (SUB // TILE) * (2 * TILE), 2 * TILE), 2 * TILE)
            total[r, c] += patch
        return carry

    tile_load.wait()
    lax.fori_loop(0, blocks // JOINT, several, 0)


def swapped(index, bits):
    result = index
    bit = 1
    while bit <= bits:
        if bits & bit:
            result = result + bit * (1 - 2 * ((index // bit) % 2))
        bit *= 2
    return result


def exchange_kernel(
    grid_count, vis_count, unitary, total, col, row, embed, scale, out,
    part, spectra, pieces, summed, gathered,
    send1, recv1, send2, recv2, send3, recv3,
):
    me_g, me_v = lax.axis_index("grid"), lax.axis_index("vis")
    groups = grid_count // NBLK
    rows_here = out.shape[0]
    quarter = CONTRIB // vis_count
    peers_v = [lax.rem(me_v + k, vis_count) for k in range(vis_count)]
    peers_g = [swapped(me_g, k) for k in range(grid_count)]
    mine = pl.ds(pl.multiple_of(me_v * rows_here, rows_here), rows_here)
    barrier = pltpu.get_barrier_semaphore()
    for k in range(grid_count - 1, 0, -1):
        pl.semaphore_signal(barrier, inc=1, device_id=(peers_g[k], me_v), device_id_type=MESH)
    for k in range(1, vis_count):
        pl.semaphore_signal(barrier, inc=1, device_id=(me_g, peers_v[k]), device_id_type=MESH)

    group = lax.broadcasted_iota(jnp.int32, (TILE, 2 * TILE), 0) // 8
    other = lax.broadcasted_iota(jnp.int32, (TILE, 2 * TILE), 1) % TILE // 8
    power = (group * group + other * other).astype(jnp.float32)
    fall = jnp.exp(power * (-64.0 / (TAPER_SCALE * TAPER_SCALE)))
    for a in range(SUB // TILE):
        for e in range(SUB // TILE):
            spot = (slice(a * TILE, (a + 1) * TILE), slice(e * 2 * TILE, (e + 1) * 2 * TILE))
            part[spot] = (total[spot] * fall).astype(jnp.bfloat16)
    for g in range(groups):
        image = jnp.dot(
            part[...], col[:, 2 * LANES * g : 2 * LANES * (g + 1)], preferred_element_type=jnp.float32
        )
        image = (image * unitary).astype(jnp.bfloat16)
        both = jnp.concatenate([image[:, :LANES], image[:, LANES:]], 0)
        result = jnp.dot(row[...], both, preferred_element_type=jnp.float32)
        result = (result * unitary).astype(jnp.bfloat16)
        spectra[:, NBLK * g : NBLK * (g + 1)] = result.reshape(vis_count, NBLK, quarter, LANES)

    pl.semaphore_wait(barrier, grid_count + vis_count - 2)

    size = grid_count // PIECES
    spots = [pl.ds(swapped(me_g // size, h) * size, size) for h in range(PIECES)]

    def copy1(h, k):
        return pltpu.make_async_remote_copy(
            src_ref=spectra.at[peers_v[k], spots[h]], dst_ref=pieces.at[k, spots[h]],
            send_sem=send1.at[h, k], recv_sem=recv1.at[h, k], device_id=(me_g, peers_v[k]), device_id_type=MESH,
        )

    def copy2(k):
        return pltpu.make_async_remote_copy(
            src_ref=summed.at[peers_g[k]], dst_ref=gathered.at[me_g, me_v], send_sem=send2.at[k],
            recv_sem=recv2.at[k], device_id=(peers_g[k], me_v), device_id_type=MESH,
        )

    def copy3(k, j):
        spot = gathered.at[peers_g[k], me_v]
        return pltpu.make_async_remote_copy(
            src_ref=spot, dst_ref=spot, send_sem=send3.at[k, j],
            recv_sem=recv3.at[k, j], device_id=(me_g, peers_v[j]), device_id_type=MESH,
        )

    for h in range(PIECES - 1, -1, -1):
        for k in range(1, vis_count):
            copy1(h, k).start()
    for h in range(PIECES - 1, -1, -1):
        whole = spectra[me_v, spots[h]].astype(jnp.float32)
        for k in range(1, vis_count):
            copy1(h, k).wait_recv()
            whole = whole + pieces[k, spots[h]].astype(jnp.float32)
        summed[spots[h]] = whole.astype(jnp.bfloat16)
        for k in range((h + 1) * size - 1, max(h * size - 1, 0), -1):
            copy2(k).start()
    gathered[me_g, me_v] = summed[me_g]
    for k in range(grid_count):
        if k > 0:
            copy2(k).wait_recv()
        for j in range(1, vis_count):
            copy3(k, j).start()
    for k in range(grid_count):
        for j in range(1, vis_count):
            copy3(k, j).wait_recv()
    sign = jnp.where(lax.broadcasted_iota(jnp.int32, (1, LANES), 1) < CONTRIB, -1.0, 1.0)
    for g in range(groups):
        straight = gathered[NBLK * g : NBLK * (g + 1)].reshape(SUB, LANES)
        turned = pltpu.roll(straight.astype(jnp.float32), CONTRIB, 1) * sign
        both = jnp.concatenate([straight, turned.astype(jnp.bfloat16)], 0)
        mixture = jnp.dot(embed[mine], both, preferred_element_type=jnp.float32)
        out[:, LANES * g : LANES * (g + 1)] = (mixture * scale[mine]).astype(jnp.bfloat16)
    for h in range(PIECES):
        for k in range(1, vis_count):
            copy1(h, k).wait_send()
    for k in range(1, grid_count):
        copy2(k).wait_send()
    for k in range(grid_count):
        for j in range(1, vis_count):
            copy3(k, j).wait_send()


def image_kernel(mixture, table, weight, out, image, save_sem):
    rows_here = mixture.shape[0]
    saves = []
    for c in range(2):
        for h in range(SAVES):
            part = slice(h * (rows_here // SAVES), (h + 1) * (rows_here // SAVES))
            result = jnp.dot(
                mixture[part], table[:, c * FAC : (c + 1) * FAC], preferred_element_type=jnp.float32
            )
            image[c, part] = result * weight[...]
            saves.append(
                pltpu.make_async_copy(
                    image.at[c, part], out.at[0, c, part], save_sem.at[c * SAVES + h]
                )
            )
            saves[-1].start()
    for save in saves:
        save.wait()


def shards(grid_count, vis_count, vis_coords, vis_values, tile_index):
    groups = grid_count // NBLK
    quarter = CONTRIB // vis_count
    rows_here = FAC // vis_count
    unitary = 1.0 / math.sqrt(SUB)
    bf16, f32 = jnp.bfloat16, jnp.float32
    far = pl.BlockSpec(memory_space=pltpu.HBM)
    inside = pl.BlockSpec(memory_space=pltpu.VMEM)
    dma = pltpu.SemaphoreType.DMA
    blocks = vis_coords.shape[1]
    visible = vis_coords.shape[3]
    partial = pl.pallas_call(
        grid_kernel,
        out_shape=jax.ShapeDtypeStruct((SUB, 2 * SUB), f32),
        in_specs=[
            far,
            far,
            far,
        ],
        out_specs=pl.BlockSpec(memory_space=pltpu.VMEM),
        scratch_shapes=[
            pltpu.SMEM((1, blocks), jnp.int32),
            pltpu.VMEM((blocks, 2, visible), f32),
            pltpu.VMEM((blocks, 2, visible), f32),
            dma,
            dma((blocks // JOINT, 2)),
        ],
        compiler_params=pltpu.CompilerParams(vmem_limit_bytes=ROOM),
        cost_estimate=pl.CostEstimate(flops=10**10, bytes_accessed=10**6, transcendentals=10**6),
        name="gridding",
    )(
        pltpu.with_memory_space_constraint(tile_index, pltpu.HBM),
        pltpu.with_memory_space_constraint(vis_coords.reshape(blocks, 2, visible), pltpu.HBM),
        pltpu.with_memory_space_constraint(vis_values.reshape(blocks, 2, visible), pltpu.HBM),
    )

    row_scale = taper() * (unitary / math.sqrt(CONTRIB * groups))
    row_scale = np.broadcast_to(row_scale[:, None], (FAC, LANES)).astype(np.float32)
    mixture = pl.pallas_call(
        functools.partial(exchange_kernel, grid_count, vis_count, unitary),
        out_shape=jax.ShapeDtypeStruct((rows_here, groups * LANES), bf16),
        in_specs=[inside] * 5,
        out_specs=pl.BlockSpec(memory_space=pltpu.VMEM),
        scratch_shapes=[
            pltpu.VMEM((SUB, 2 * SUB), bf16),
            pltpu.VMEM((vis_count, grid_count, quarter, LANES), bf16),
            pltpu.VMEM((vis_count, grid_count, quarter, LANES), bf16),
            pltpu.VMEM((grid_count, quarter, LANES), bf16),
            pltpu.VMEM((grid_count, vis_count, quarter, LANES), bf16),
            dma((PIECES, vis_count)),
            dma((PIECES, vis_count)),
            dma((grid_count,)),
            dma((grid_count,)),
            dma((grid_count, vis_count)),
            dma((grid_count, vis_count)),
        ],
        compiler_params=pltpu.CompilerParams(
            collective_id=0, has_side_effects=True, vmem_limit_bytes=ROOM
        ),
        cost_estimate=pl.CostEstimate(flops=10**10, bytes_accessed=10**6, transcendentals=0),
        name="exchange",
    )(
        partial,
        jnp.asarray(column_table(groups)),
        jnp.asarray(row_table(vis_count)),
        jnp.asarray(embed_table()),
        jnp.asarray(row_scale),
    )

    return pl.pallas_call(
        image_kernel,
        out_shape=jax.ShapeDtypeStruct((1, 2, rows_here, FAC), f32),
        in_specs=[inside] * 3,
        out_specs=far,
        scratch_shapes=[pltpu.VMEM((2, rows_here, FAC), f32), dma((2 * SAVES,))],
        compiler_params=pltpu.CompilerParams(vmem_limit_bytes=ROOM),
        name="images",
    )(
        mixture,
        jnp.asarray(output_table(groups)),
        jnp.asarray(taper()[None, :].astype(np.float32)),
    )


def solution(mesh):
    placed = (P("grid", "vis", None, None), P("grid", "vis", None, None), P("grid", "vis"))
    body = functools.partial(shards, mesh.shape["grid"], mesh.shape["vis"])
    return jax.shard_map(
        body, mesh=mesh, in_specs=placed, out_specs=P("grid", None, "vis", None), check_vma=False
    )
```
